32 devices in a mesh: groups: 2 (over y), expert: 4 (over x, core), hidden: 4 (over z).
Axes of the slice: x: 2, y: 2, z: 4, core: 2. Of those that a mesh axis runs over, the one named last changes fastest.
Arguments:
- tokens: bfloat16 [1024, 3072], P(('groups', 'expert'), 'hidden'), parts along dimension 0, may hold values from -6 to 6
- routes: int32 [1024, 2], P(('groups', 'expert')), parts along dimension 0, may hold values from 0 to 7, all different within a row; in each aligned block of 128 rows (0 to 127, 128 to 255, ...) at most 48 rows name the same one
- router_weight: bfloat16 [3072, 8], replicated, may hold values from -0.109375 to 0.109375
- gate_weight: bfloat16 [8, 3072, 8192], P('expert', None, 'hidden'), may hold values from -0.109375 to 0.109375
- up_weight: bfloat16 [8, 3072, 8192], P('expert', None, 'hidden'), may hold values from -0.109375 to 0.109375
- down_weight: bfloat16 [8, 8192, 3072], P('expert', 'hidden'), may hold values from -0.09375 to 0.09375
Outputs:
- mixed: bfloat16 [1024, 3072], P(('groups', 'expert'), 'hidden'), parts along dimension 0
The draws below stay inside these ranges and needn't reach their ends.
There are 2 independent parts, one for each index of `groups`. The reference program is written for one: setup_inputs(seed, part) draws one part's arguments, and reference() takes and returns one part's arrays. A program takes and returns all parts, laid end to end along the dimension named above; an argument that names none is the same for every part. Nothing has to cross between parts.
Inputs may be any that keep to these rules, and one draw needn't show every extreme that they name: `routes`: each token names two different experts. Among the 128 tokens of one index of expert (aligned blocks of rows) no expert is named more than 48 times, a bound that some block reaches.
All inputs are finite; a program needn't handle non-finite values.
Results may differ from the reference program's by a relative error of at most 0.0057.
Values may be sent and summed in bfloat16 or wider, within the bound.
No kernel may reach another device: no remote copies, remote signals or barrier semaphores. Data moves between devices by JAX's collectives and lax.ppermute only.
A program may use at most 128 MiB of HBM per device.

```python
import math
import jax
import jax.numpy as jnp
import numpy as np
from jax import lax

D = 3072
FF = 8192
EXPERTS = 8
TOP = 2
TOK_E = 128
CAP = 48
TOKENS = 512
N_EXPERT = 4


def raised(drawn, key, source, target, parts, factor):
    def block_of(dim):
        return (jnp.arange(drawn.shape[dim]) // (drawn.shape[dim] // parts)).reshape((-1,) + (1,) * (drawn.ndim - 1 - dim))

    one_side = jax.random.permutation(key, parts)[block_of(target)]
    second = (block_of(target) + parts // 2) % parts
    return jnp.where((block_of(source) == one_side) | (block_of(source) == second), factor * drawn, drawn)


def steps_of(own_key, dims, split, smallest, largest):
    def one(axis_at, shards_of):
        draws = jax.random.uniform(jax.random.fold_in(jax.random.fold_in(own_key, 6), axis_at), (shards_of,), jnp.float32, smallest / len(split), largest / len(split))
        return jnp.repeat(jnp.exp(draws), dims[axis_at] // shards_of).reshape((-1,) + (1,) * (len(dims) - axis_at - 1))

    factor_of = one(*split[0])
    for cut in split[1:]:
        factor_of = factor_of * one(*cut)
    return factor_of


def assign_block(key, own, number, rows, amount, top, most, lean):
    ranking = jax.random.permutation(key, amount)
    packed, usual = load_shares(amount, rows * top, most, lean, True), load_shares(amount, rows * top, most, lean, False)
    places = jnp.arange(amount)

    def named(sizes, turn):
        used = int((sizes > 0).sum())
        fixed = max(1, used // 4)
        shifted = fixed + (places - fixed + turn * (used - fixed)) % max(1, amount - fixed)
        return jnp.zeros((amount,), jnp.int32).at[ranking[jnp.where(places < fixed, places, shifted)]].set(jnp.asarray(sizes, jnp.int32))

    sizes = jnp.where(number % 4 == 0, named(packed, number // 4), named(usual, number - number // 4 - 1))
    mixed = jax.random.permutation(jax.random.fold_in(own, 3), amount)
    donor, sink = mixed[0:amount // 2 * 2:2], mixed[1:amount // 2 * 2:2]
    room = jnp.minimum(sizes[donor] - 1, most - sizes[sink]) // 2
    room = jnp.where((donor == ranking[0]) | (sink == ranking[0]) | (sizes[sink] == 0), 0, jnp.maximum(room, 0))
    shifted = jax.random.randint(jax.random.fold_in(own, 4), (amount // 2,), 0, 1 << 20) % (room + 1)
    sizes = sizes.at[donor].add(-shifted).at[sink].add(shifted)
    members = jnp.searchsorted(jnp.cumsum(sizes), jnp.arange(rows * top), side="right").astype(jnp.int32)
    listing = members.reshape(top, rows).T
    listing = listing[jax.random.permutation(jax.random.fold_in(own, 1), rows)]
    turn = jax.random.randint(jax.random.fold_in(own, 2), (rows, 1), 0, top)
    return jnp.take_along_axis(listing, (jnp.arange(top)[None, :] + turn) % top, axis=1)


def load_shares(count, total, most, lean, full):
    weights = [(1 << 20) // math.isqrt(rank ** lean) + 1 for rank in range(1, count + 1)]
    largest = most if full else min(most, max(-(-total // count), total * weights[0] // sum(weights)))
    least = 1 if total - largest >= count - 1 else 0
    counts, surplus = [largest] + [least] * (count - 1), total - largest - least * (count - 1)
    while surplus > 0:
        free = [i for i in range(1, count) if counts[i] < largest] or [i for i in range(1, count) if counts[i] < most]
        pool, budget = sum([weights[i] for i in free]), surplus
        for i in free:
            extra = min(most - counts[i], max(1, budget * weights[i] // pool), surplus)
            counts[i] = counts[i] + extra
            surplus = surplus - extra
    return np.array(counts)


def noise(key, dims, deviation, limit, shards=(), held_as=jnp.bfloat16):
    values = jax.random.normal(key, dims, jnp.float32) * deviation
    if len(shards) > 0:
        values = steps_of(key, dims, shards, -0.22, 0.18) * values
    return jnp.clip(values, min=-limit, max=limit).astype(held_as)


def bell_draw_with(rng, shape, scale, bound, shards, heavy, held_as=jnp.bfloat16):
    result = scale * jax.random.normal(rng, shape, jnp.float32)
    if shards:
        result = result * steps_of(rng, shape, shards, -0.22, 0.18)
    return jnp.clip(raised(result, jax.random.fold_in(rng, 3), *heavy), -bound, bound).astype(held_as)


def setup_inputs(seed: int = 0, part: int = 0) -> dict:
    seeds = jax.random.split(jax.random.key(seed), 7)
    part_keys = jax.random.split(jax.random.fold_in(seeds[6], part), 7)
    tokens = noise(part_keys[0], (TOKENS, D), 1.0, 6.0, ((0, 4), (1, 4)))
    routes_keys = jax.random.split(jax.random.fold_in(part_keys[1], 1), TOKENS // TOK_E)
    routes_turns = jax.random.permutation(jax.random.fold_in(part_keys[1], 3), TOKENS // TOK_E)
    routes = jax.vmap(lambda own, number: assign_block(jax.random.fold_in(part_keys[1], 2), own, number, TOK_E, EXPERTS, 2, CAP, 2))(routes_keys, routes_turns).reshape((TOKENS, TOP))
    router_weight = noise(seeds[2], (D, EXPERTS), D ** -0.5, 0.109375)
    gate_weight = noise(seeds[3], (EXPERTS, D, FF), D ** -0.5, 0.109375, ((0, 4), (2, 4)))
    up_weight = noise(seeds[4], (EXPERTS, D, FF), D ** -0.5, 0.109375, ((0, 4), (2, 4)))
    down_weight = bell_draw_with(seeds[5], (EXPERTS, FF, D), FF ** -0.5, 0.09375, ((0, 4), (1, 4)), (1, 2, 4, 2.0))
    return {"tokens": tokens, "routes": routes, "router_weight": router_weight, "gate_weight": gate_weight, "up_weight": up_weight, "down_weight": down_weight}


def expert_rows(inputs):
    gathered, w_gate, w_up, w_down = inputs
    gate_act = jnp.dot(gathered, w_gate, preferred_element_type=jnp.float32)
    up_act = jnp.dot(gathered, w_up, preferred_element_type=jnp.float32)
    hidden_act = (jax.nn.silu(gate_act) * up_act).astype(jnp.bfloat16)
    return jnp.dot(hidden_act, w_down, preferred_element_type=jnp.float32).astype(jnp.bfloat16)


def reference(tokens, routes, router_weight, gate_weight, up_weight, down_weight):
    slots_all = N_EXPERT * CAP
    flat_ids = routes.reshape(N_EXPERT, TOK_E * 2)
    onehot = (flat_ids[:, :, None] == jnp.arange(EXPERTS, dtype=jnp.int32)[None, None, :]).astype(jnp.int32)
    position = jnp.sum((jnp.cumsum(onehot, axis=1) - onehot) * onehot, axis=2)
    source = jnp.arange(N_EXPERT, dtype=jnp.int32)[:, None]
    slot_of = (flat_ids * slots_all + source * CAP + position).reshape(-1).astype(jnp.int32)
    owners = (jnp.arange(TOKENS * 2, dtype=jnp.int32) // 2).astype(jnp.int32)
    inverse = jnp.full((EXPERTS * slots_all,), TOKENS, jnp.int32).at[slot_of].set(owners)
    padded = jnp.concatenate([tokens, jnp.zeros((1, D), jnp.bfloat16)], axis=0)
    inverse = inverse.reshape(EXPERTS, slots_all)
    outputs = lax.map(lambda item: expert_rows((padded[item[0]], item[1], item[2], item[3])),
                      (inverse, gate_weight, up_weight, down_weight))
    outputs = outputs.reshape(EXPERTS * slots_all, D)
    logits = jnp.dot(tokens, router_weight, preferred_element_type=jnp.float32)
    selected = jnp.take_along_axis(logits, routes, axis=1)
    share = jax.nn.sigmoid(selected[:, 0] - selected[:, 1])
    slot_pairs = slot_of.reshape(TOKENS, 2)
    first_out = outputs[slot_pairs[:, 0]].astype(jnp.float32)
    second_out = outputs[slot_pairs[:, 1]].astype(jnp.float32)
    mixture = share[:, None] * first_out + (1.0 - share)[:, None] * second_out
    return mixture.astype(jnp.bfloat16)
```

```python
import functools
import jax
import jax.numpy as jnp
from jax import lax
from jax.experimental import pallas as pl
from jax.experimental.pallas import tpu as pltpu
from jax.sharding import PartitionSpec as P

CAP = 48
f32, bf16 = jnp.float32, jnp.bfloat16
VM = pl.BlockSpec(memory_space=pltpu.VMEM)
ANY = pl.BlockSpec(memory_space=pl.ANY)


def silu_mul(gate, up):
    return (jax.nn.silu(gate) * up).astype(bf16)


def up_kernel(first, last, blocks, experts, parts, *refs):
    idx, refs = refs[0], list(refs[1:])
    xs, refs = refs[:blocks], refs[blocks:]
    sel, router, wg, wu = refs[:4]
    refs = refs[4:]
    if not first:
        g_in, u_in, l_in = refs[:3]
        refs = refs[3:]
    if last:
        h_out, l_out = refs[:2]
        refs = refs[2:]
    else:
        g_out, u_out, l_out = refs[:3]
        refs = refs[3:]
    rows, buf, sem = refs
    kb = rows.shape[2]
    sub = kb // parts
    base = idx[0] * kb
    copies = []
    for e in range(experts):
        for m, w in enumerate((wg, wu)):
            for p in range(parts):
                at = pl.ds(pl.multiple_of(base + p * sub, 8), sub)
                copies.append(
                    pltpu.make_async_copy(
                        w.at[e, at], buf.at[e, m, pl.ds(p * sub, sub)], sem.at[e, m, p]
                    )
                )
    for c in copies:
        c.start()
    rt = router[:, pl.ds(pl.multiple_of(base, 128), kb)]
    for j in range(blocks):
        x = xs[j][...]
        got = jnp.dot(sel[j], x, preferred_element_type=f32).astype(bf16)
        for e in range(experts):
            rows[e, j * CAP : (j + 1) * CAP] = got[e * CAP : (e + 1) * CAP]
        lt = lax.dot_general(rt, x, (((1,), (1,)), ((), ())), preferred_element_type=f32)
        l_out[j] = lt if first else l_in[j] + lt
    n_all = wg.shape[2]
    step = min(512, n_all)
    for e in range(experts):
        x = rows[e]
        waits = copies[e * 2 * parts : (e + 1) * 2 * parts]
        if last:
            for c in waits:
                c.wait()
            for n in range(0, n_all, step):
                sl = slice(n, n + step)
                g = g_in[e, :, sl] + jnp.dot(x, buf[e, 0, :, sl], preferred_element_type=f32)
                u = u_in[e, :, sl] + jnp.dot(x, buf[e, 1, :, sl], preferred_element_type=f32)
                h_out[e, :, sl] = silu_mul(g, u)
            continue
        for m in range(2):
            for c in waits[m * parts : (m + 1) * parts]:
                c.wait()
            for n in range(0, n_all, step):
                sl = slice(n, n + step)
                v = jnp.dot(x, buf[e, m, :, sl], preferred_element_type=f32)
                (g_out, u_out)[m][e, :, sl] = v if first else (g_in, u_in)[m][e, :, sl] + v


def up_chunk(block, xs, sel, router, wg, wu, acc, last):
    experts, _, ff = wg.shape
    blocks = len(xs)
    kb = xs[0].shape[1]
    slots = blocks * CAP
    first = acc is None
    parts = 2
    big = jax.ShapeDtypeStruct((experts, slots, ff), f32)
    lo = jax.ShapeDtypeStruct((blocks, router.shape[0], xs[0].shape[0]), f32)
    out = (jax.ShapeDtypeStruct((experts, slots, ff), bf16), lo) if last else (big, big, lo)
    args = [block.reshape(1).astype(jnp.int32), *xs, sel, router, wg, wu] + ([] if first else list(acc))
    n0 = 1 + blocks + 4
    alias = {} if first else ({n0 + 2: 1} if last else {n0: 0, n0 + 1: 1, n0 + 2: 2})
    return pl.pallas_call(
        functools.partial(up_kernel, first, last, blocks, experts, parts),
        out_shape=out,
        in_specs=[pl.BlockSpec(memory_space=pltpu.SMEM)] + [VM] * blocks + [VM, VM, ANY, ANY] + ([] if first else [VM] * 3),
        out_specs=tuple([VM] * len(out)),
        scratch_shapes=[
            pltpu.VMEM((experts, slots, kb), bf16),
            pltpu.VMEM((experts, 2, kb, ff), bf16),
            pltpu.SemaphoreType.DMA((experts, 2, parts)),
        ],
        input_output_aliases=alias,
        compiler_params=pltpu.CompilerParams(vmem_limit_bytes=32 << 20),
        cost_estimate=pl.CostEstimate(
            flops=4 * experts * slots * kb * ff,
            bytes_accessed=4 * experts * kb * ff,
            transcendentals=experts * slots * ff if last else 0,
        ),
    )(*args)


def up_chunk_plain(block, xs, sel, router, wg, wu, acc, last):
    kb, experts, blocks = xs[0].shape[1], wg.shape[0], len(xs)
    x = jnp.stack(xs)
    rows = jnp.einsum("jst,jtd->jsd", sel, x, preferred_element_type=f32).astype(bf16)
    rows = rows.reshape(blocks, experts, CAP, kb).swapaxes(0, 1).reshape(experts, blocks * CAP, kb)
    cut = lambda w: lax.dynamic_slice_in_dim(w, block * kb, kb, axis=1)
    g = jnp.einsum("erd,edf->erf", rows, cut(wg), preferred_element_type=f32)
    u = jnp.einsum("erd,edf->erf", rows, cut(wu), preferred_element_type=f32)
    lo = jnp.einsum("nd,jtd->jnt", cut(router), x, preferred_element_type=f32)
    if acc is not None:
        g, u, lo = g + acc[0], u + acc[1], lo + acc[2]
    return (silu_mul(g, u), lo) if last else (g, u, lo)


def down_kernel(experts, blocks, parts, idx, h_ref, back, wslot, wd, keep, send, part, buf, sem):
    kb = part.shape[2]
    ff = wd.shape[1]
    sub = ff // parts
    col = pl.ds(pl.multiple_of(idx[0] * kb, 128), kb)
    copies = []
    for e in range(experts):
        for p in range(parts):
            copies.append(
                pltpu.make_async_copy(
                    wd.at[e, pl.ds(p * sub, sub), col], buf.at[e, pl.ds(p * sub, sub)], sem.at[e, p]
                )
            )
    for c in copies:
        c.start()
    at = 0
    for e in range(experts):
        v = None
        for p in range(parts):
            copies[at].wait()
            at += 1
            d = jnp.dot(h_ref[e, :, p * sub : (p + 1) * sub], buf[e, p * sub : (p + 1) * sub], preferred_element_type=f32)
            v = d if v is None else v + d
        v = (v * wslot[e]).astype(bf16)
        for j in range(blocks):
            part[j, e * CAP : (e + 1) * CAP] = v[j * CAP : (j + 1) * CAP]
    for j in range(blocks):
        y = jnp.dot(back[j], part[j], preferred_element_type=f32).astype(bf16)
        if j % 2 == 0:
            keep[j // 2] = y
        else:
            send[j // 2] = y


def down_chunk(block, h, back, wslot, wd, kb):
    experts, slots, ff = h.shape
    blocks, toks, _ = back.shape
    out = jax.ShapeDtypeStruct((blocks // 2, toks, kb), bf16)
    parts = 2
    return pl.pallas_call(
        functools.partial(down_kernel, experts, blocks, parts),
        out_shape=(out, out),
        in_specs=[pl.BlockSpec(memory_space=pltpu.SMEM), VM, VM, VM, ANY],
        out_specs=(VM, VM),
        scratch_shapes=[
            pltpu.VMEM((blocks, experts * CAP, kb), bf16),
            pltpu.VMEM((experts, ff, kb), bf16),
            pltpu.SemaphoreType.DMA((experts, parts)),
        ],
        compiler_params=pltpu.CompilerParams(vmem_limit_bytes=20 << 20),
        cost_estimate=pl.CostEstimate(
            flops=2 * experts * slots * kb * ff, bytes_accessed=2 * experts * kb * ff, transcendentals=0
        ),
    )(block.reshape(1).astype(jnp.int32), h, back, wslot, wd)


def down_chunk_plain(block, h, back, wslot, wd, kb):
    experts, slots, ff = h.shape
    blocks, toks, _ = back.shape
    w = lax.dynamic_slice_in_dim(wd, block * kb, kb, axis=2)
    v = jnp.einsum("erf,efd->erd", h, w, preferred_element_type=f32)
    v = (v * wslot).astype(bf16).reshape(experts, blocks, CAP, kb).swapaxes(0, 1).reshape(blocks, experts * CAP, kb)
    y = jnp.einsum("jts,jsd->jtd", back, v, preferred_element_type=f32).astype(bf16)
    y = y.reshape(blocks // 2, 2, toks, kb)
    return y[:, 0], y[:, 1]


def per_device(tokens, routes, router_weight, gate_weight, up_weight, down_weight):
    experts = gate_weight.shape[0]
    blocks = lax.axis_size("expert")
    nh = lax.axis_size("hidden")
    chips = blocks // 2
    toks, kb = tokens.shape
    e_at = lax.axis_index("expert")
    h_at = lax.axis_index("hidden")
    over_core = lambda v: lax.ppermute(v, "expert", [(i, i ^ 1) for i in range(blocks)])
    over_x = lambda v, d: lax.ppermute(v, "expert", [(i, i ^ (2 * d)) for i in range(blocks)])
    over_z = lambda v, k: lax.ppermute(v, "hidden", [(i, i ^ k) for i in range(nh)])

    def spread(v):
        evens = [v] + [over_x(v, d) for d in range(1, chips)]
        return [w for v in evens for w in (v, over_core(v))]

    slices = [tokens] + [over_z(tokens, k) for k in range(1, nh)]
    names = jnp.stack(spread(routes.T))

    here = e_at * experts + jnp.arange(experts, dtype=jnp.int32)
    mine = (names[:, None, :, :] == here[None, :, None, None]).any(axis=2)
    ahead = (jnp.arange(toks)[:, None] < jnp.arange(toks)[None, :]).astype(bf16)
    rank = jnp.dot(mine.astype(bf16).reshape(blocks * experts, toks), ahead, preferred_element_type=f32)
    rank = rank.astype(jnp.int32).reshape(blocks, experts, 1, toks)
    sel = (mine[:, :, None, :] & (rank == jnp.arange(CAP, dtype=jnp.int32)[None, None, :, None]))
    sel16 = sel.astype(bf16).reshape(blocks, experts * CAP, toks)
    back = sel16.swapaxes(1, 2)

    router = router_weight.T
    kernels = kb % 128 == 0 and toks % 128 == 0
    acc = None
    for k in range(nh):
        xs = spread(slices[k])
        if kernels:
            acc = up_chunk(h_at ^ k, xs, sel16, router, gate_weight, up_weight, acc, k == nh - 1)
        else:
            acc = up_chunk_plain(h_at ^ k, xs, sel16, router, gate_weight, up_weight, acc, k == nh - 1)
    h, logits = acc

    num = jnp.arange(logits.shape[1], dtype=jnp.int32)[None, None, :, None]
    own = here[None, :, None, None]
    other = jnp.sum(names, axis=1)[:, None, None, :] - own
    sign = (num == own).astype(f32) - (num == other).astype(f32)
    weight = jax.nn.sigmoid(jnp.sum(sign * logits[:, None], axis=2))
    wslot = jnp.sum(jnp.where(sel, weight[:, :, None, :], 0.0), axis=3)
    wslot = wslot.swapaxes(0, 1).reshape(experts, blocks * CAP, 1)

    total = None
    order = [k for k in range(nh - 1, 0, -1)] + [0]
    for k in order:
        fn = down_chunk if kernels else down_chunk_plain
        keep, send = fn(h_at ^ k, h, back, wslot, down_weight, kb)
        both = keep.astype(f32) + over_core(send).astype(f32)
        mid = both[0]
        for d in range(1, chips):
            mid = mid + over_x(both[d].astype(bf16), d).astype(f32)
        if k:
            mid = over_z(mid.astype(bf16), k).astype(f32)
        total = mid if total is None else total + mid
    return total.astype(bf16)


def solution(mesh):
    return jax.shard_map(
        per_device,
        mesh=mesh,
        in_specs=(
            P(("groups", "expert"), "hidden"),
            P(("groups", "expert"), None),
            P(),
            P("expert", None, "hidden"),
            P("expert", None, "hidden"),
            P("expert", "hidden", None),
        ),
        out_specs=P(("groups", "expert"), "hidden"),
        check_vma=False,
    )
```

```python
import functools
import jax
import jax.numpy as jnp
from jax import lax
from jax.experimental import pallas as pl
from jax.experimental.pallas import tpu as pltpu
from jax.sharding import PartitionSpec as P


CAP = 48
f32, bf16 = jnp.float32, jnp.bfloat16
VM = pl.BlockSpec(memory_space=pltpu.VMEM)
ANY = pl.BlockSpec(memory_space=pltpu.HBM)
SM = pl.BlockSpec(memory_space=pltpu.SMEM)


def silu_mul(gate, up):
    return (jax.nn.silu(gate) * up).astype(bf16)


def plan_kernel(blocks, experts, idx, *refs):
    names, (sel_out, back_out, sign_out) = refs[:blocks], refs[blocks:]
    toks = names[0].shape[1]
    ahead = (lax.broadcasted_iota(jnp.int32, (toks, toks), 1) < lax.broadcasted_iota(jnp.int32, (toks, toks), 0)).astype(bf16)
    row = lax.broadcasted_iota(jnp.int32, (CAP, toks), 0)
    col = lax.broadcasted_iota(jnp.int32, (toks, CAP), 1)
    num = lax.broadcasted_iota(jnp.int32, (sign_out.shape[2], toks), 0)
    contract = (((1,), (1,)), ((), ()))
    for j in range(blocks):
        pair = names[j][...]
        for e in range(experts):
            own = idx[0] + e
            mine = (pair[0:1] == own) | (pair[1:2] == own)
            flag = mine.astype(f32)
            wide = jnp.broadcast_to(flag, (8, toks)).astype(bf16)
            rank = lax.dot_general(wide, ahead, contract, preferred_element_type=f32)[0:1]
            rank = jnp.where(mine, rank, -1.0).astype(jnp.int32)
            sel_out[j, e * CAP : (e + 1) * CAP] = (rank == row).astype(f32).astype(bf16)
            deep = lax.dot_general(ahead, wide, contract, preferred_element_type=f32)[:, 0:1]
            eye = (lax.broadcasted_iota(jnp.int32, (toks, toks), 1) == lax.broadcasted_iota(jnp.int32, (toks, toks), 0)).astype(bf16)
            held = lax.dot_general(eye, wide, contract, preferred_element_type=f32)[:, 0:1]
            deep = jnp.where(held > 0.5, deep, -1.0).astype(jnp.int32)
            back_out[j, :, e * CAP : (e + 1) * CAP] = (deep == col).astype(f32).astype(bf16)
            other = pair[0:1] + pair[1:2] - own
            sign_out[j, e] = (num == own).astype(f32) - (num == other).astype(f32)


def plan(base, names, experts, count):
    blocks, toks = len(names), names[0].shape[1]
    return pl.pallas_call(
        functools.partial(plan_kernel, blocks, experts),
        out_shape=(
            jax.ShapeDtypeStruct((blocks, experts * CAP, toks), bf16),
            jax.ShapeDtypeStruct((blocks, toks, experts * CAP), bf16),
            jax.ShapeDtypeStruct((blocks, experts, count, toks), f32),
        ),
        in_specs=[SM] + [VM] * blocks,
        out_specs=(VM, VM, VM),
        compiler_params=pltpu.CompilerParams(vmem_limit_bytes=4 << 20),
        cost_estimate=pl.CostEstimate(flops=1 << 24, bytes_accessed=1 << 18, transcendentals=0),
    )(base.reshape(1).astype(jnp.int32), *names)


def plan_plain(base, names, experts, count):
    names = jnp.stack(names)
    blocks, _, toks = names.shape
    here = base + jnp.arange(experts, dtype=jnp.int32)
    mine = (names[:, None, :, :] == here[None, :, None, None]).any(axis=2)
    before = (jnp.arange(toks)[:, None] < jnp.arange(toks)[None, :]).astype(bf16)
    rank = jnp.dot(mine.astype(bf16).reshape(blocks * experts, toks), before, preferred_element_type=f32)
    rank = rank.astype(jnp.int32).reshape(blocks, experts, 1, toks)
    sel = mine[:, :, None, :] & (rank == jnp.arange(CAP, dtype=jnp.int32)[None, None, :, None])
    sel = sel.astype(bf16).reshape(blocks, experts * CAP, toks)
    num = jnp.arange(count, dtype=jnp.int32)[None, None, :, None]
    own = here[None, :, None, None]
    other = jnp.sum(names, axis=1)[:, None, None, :] - own
    return sel, sel.swapaxes(1, 2), (num == own).astype(f32) - (num == other).astype(f32)


def fetch_up(wg, wu, block, kb, out, sem):
    at = pl.ds(pl.multiple_of(block * kb, 128), kb)
    copies = []
    for e in range(wg.shape[0]):
        for m, w in enumerate((wg, wu)):
            copies.append(pltpu.make_async_copy(w.at[e, at], out.at[e, m], sem.at[e, m]))
    return copies


def fetch_down(wd, block, kb, out, sem):
    col = pl.ds(pl.multiple_of(block * kb, 128), kb)
    half = wd.shape[1] // 2
    copies = []
    for e in range(wd.shape[0]):
        for p in range(2):
            rows = pl.ds(p * half, half)
            copies.append(pltpu.make_async_copy(wd.at[e, rows, col], out.at[e, rows], sem.at[e, p]))
    return copies


def first_kernel(idx, tokens, router, wg, wu, tok_out, router_out, w_out, sem, small):
    copies = [
        pltpu.make_async_copy(tokens, tok_out, small.at[0]),
        pltpu.make_async_copy(router, router_out, small.at[1]),
    ] + fetch_up(wg, wu, idx[0], tokens.shape[1], w_out, sem)
    for c in copies:
        c.start()
    for c in copies:
        c.wait()


def first_fetch(block, tokens, router, wg, wu):
    experts, _, ff = wg.shape
    kb = tokens.shape[1]
    return pl.pallas_call(
        first_kernel,
        out_shape=(
            jax.ShapeDtypeStruct(tokens.shape, bf16),
            jax.ShapeDtypeStruct(router.shape, bf16),
            jax.ShapeDtypeStruct((experts, 2, kb, ff), bf16),
        ),
        in_specs=[SM, ANY, ANY, ANY, ANY],
        out_specs=(VM, VM, VM),
        scratch_shapes=[pltpu.SemaphoreType.DMA((experts, 2)), pltpu.SemaphoreType.DMA((2,))],
        compiler_params=pltpu.CompilerParams(vmem_limit_bytes=1 << 20),
        cost_estimate=pl.CostEstimate(flops=0, bytes_accessed=4 * experts * kb * ff, transcendentals=0),
    )(block.reshape(1).astype(jnp.int32), tokens, router, wg, wu)


def up_kernel(first, last, blocks, experts, *refs):
    idx, refs = refs[0], list(refs[1:])
    xs, refs = refs[:blocks], refs[blocks:]
    sel, router, now = refs[:3]
    ahead = refs[3:4] if last else refs[3:5]
    refs = refs[4:] if last else refs[5:]
    if not first:
        g_in, u_in, l_in = refs[:3]
        refs = refs[3:]
    if last:
        sign, h_out, s_out, w_out = refs[:4]
        refs = refs[4:]
    else:
        g_out, u_out, l_out, w_out = refs[:4]
        refs = refs[4:]
    rows, sem = refs
    kb = rows.shape[2]
    fetch = fetch_down if last else fetch_up
    copies = fetch(*ahead, idx[1], kb, w_out, sem)
    for c in copies:
        c.start()
    rt = router[:, pl.ds(pl.multiple_of(idx[0] * kb, 128), kb)]
    for j in range(blocks):
        x = xs[j][...]
        got = jnp.dot(sel[j], x, preferred_element_type=f32).astype(bf16)
        for e in range(experts):
            rows[e, j * CAP : (j + 1) * CAP] = got[e * CAP : (e + 1) * CAP]
        lt = lax.dot_general(rt, x, (((1,), (1,)), ((), ())), preferred_element_type=f32)
        lt = lt if first else l_in[j] + lt
        if not last:
            l_out[j] = lt
            continue
        for e in range(experts):
            w = jax.nn.sigmoid(jnp.sum(sign[j, e] * lt, axis=0, keepdims=True))
            at = sel[j, e * CAP : (e + 1) * CAP].astype(f32)
            s_out[e, j * CAP : (j + 1) * CAP] = jnp.sum(at * w, axis=1, keepdims=True)
    n_all = now.shape[3]
    step = min(512, n_all)

    def column(i, carry):
        e = i // (n_all // step)
        sl = pl.ds(pl.multiple_of(i % (n_all // step) * step, step), step)
        x = rows[e]
        g = jnp.dot(x, now[e, 0, :, sl], preferred_element_type=f32)
        u = jnp.dot(x, now[e, 1, :, sl], preferred_element_type=f32)
        if not first:
            g = g_in[e, :, sl] + g
            u = u_in[e, :, sl] + u
        if last:
            h_out[e, :, sl] = silu_mul(g, u)
        else:
            g_out[e, :, sl] = g
            u_out[e, :, sl] = u
        return carry

    lax.fori_loop(0, experts * (n_all // step), column, 0)
    for c in copies:
        c.wait()


def up_chunk(block, after, xs, sel, sign, router, now, ahead, acc, last):
    experts, _, kb, ff = now.shape
    blocks = len(xs)
    slots = blocks * CAP
    first = acc is None
    big = jax.ShapeDtypeStruct((experts, slots, ff), f32)
    lo = jax.ShapeDtypeStruct((blocks, router.shape[0], xs[0].shape[0]), f32)
    if last:
        out = (
            jax.ShapeDtypeStruct((experts, slots, ff), bf16),
            jax.ShapeDtypeStruct((experts, slots, 1), f32),
            jax.ShapeDtypeStruct((experts, ff, kb), bf16),
        )
    else:
        out = (big, big, lo, jax.ShapeDtypeStruct(now.shape, bf16))
    idx = jnp.stack([block, after]).astype(jnp.int32)
    args = [idx, *xs, sel, router, now, *ahead] + ([] if first else list(acc)) + ([sign] if last else [])
    n0 = 1 + blocks + 3 + len(ahead)
    alias = {} if first or last else {n0: 0, n0 + 1: 1, n0 + 2: 2}
    return pl.pallas_call(
        functools.partial(up_kernel, first, last, blocks, experts),
        out_shape=out,
        in_specs=[SM] + [VM] * blocks + [VM] * 3 + [ANY] * len(ahead) + ([] if first else [VM] * 3) + ([VM] if last else []),
        out_specs=tuple([VM] * len(out)),
        scratch_shapes=[pltpu.VMEM((experts, slots, kb), bf16), pltpu.SemaphoreType.DMA((experts, 2))],
        input_output_aliases=alias,
        compiler_params=pltpu.CompilerParams(vmem_limit_bytes=2 << 20),
        cost_estimate=pl.CostEstimate(
            flops=4 * experts * slots * kb * ff,
            bytes_accessed=4 * experts * kb * ff,
            transcendentals=experts * slots * ff if last else 0,
        ),
    )(*args)


def up_chunk_plain(block, xs, sel, sign, router, wg, wu, acc, last):
    kb, experts, blocks = xs[0].shape[1], wg.shape[0], len(xs)
    x = jnp.stack(xs)
    rows = jnp.einsum("jst,jtd->jsd", sel, x, preferred_element_type=f32).astype(bf16)
    rows = rows.reshape(blocks, experts, CAP, kb).swapaxes(0, 1).reshape(experts, blocks * CAP, kb)
    cut = lambda w: lax.dynamic_slice_in_dim(w, block * kb, kb, axis=1)
    g = jnp.einsum("erd,edf->erf", rows, cut(wg), preferred_element_type=f32)
    u = jnp.einsum("erd,edf->erf", rows, cut(wu), preferred_element_type=f32)
    lo = jnp.einsum("nd,jtd->jnt", cut(router), x, preferred_element_type=f32)
    if acc is not None:
        g, u, lo = g + acc[0], u + acc[1], lo + acc[2]
    if not last:
        return g, u, lo
    weight = jax.nn.sigmoid(jnp.sum(sign * lo[:, None], axis=2))
    at = sel.astype(f32).reshape(blocks, experts, CAP, -1)
    wslot = jnp.sum(at * weight[:, :, None, :], axis=3).swapaxes(0, 1)
    return silu_mul(g, u), wslot.reshape(experts, blocks * CAP, 1)


def down_kernel(experts, blocks, last, *refs):
    idx, h_ref, back, wslot, now, _ = refs[:6]
    if last:
        keep, send, part = refs[6:]
        copies = []
    else:
        wd, keep, send, w_out, part, sem = refs[6:]
        copies = fetch_down(wd, idx[0], part.shape[2], w_out, sem)
    for c in copies:
        c.start()

    def product(e, carry):
        v = jnp.dot(h_ref[e], now[e], preferred_element_type=f32)
        v = (v * wslot[e]).astype(bf16)
        at = pl.ds(pl.multiple_of(e * CAP, CAP), CAP)
        for j in range(blocks):
            part[j, at] = v[j * CAP : (j + 1) * CAP]
        return carry

    lax.fori_loop(0, experts, product, 0)
    for j in range(blocks):
        y = jnp.dot(back[j], part[j], preferred_element_type=f32).astype(bf16)
        if j % 2 == 0:
            keep[j // 2] = y
        else:
            send[j // 2] = y
    for c in copies:
        c.wait()


def down_chunk(after, h, back, wslot, now, wd, gate):
    experts, slots, ff = h.shape
    blocks, toks, _ = back.shape
    kb = now.shape[2]
    last = after is None
    out = (jax.ShapeDtypeStruct((blocks // 2, toks, kb), bf16),) * 2
    args = [jnp.zeros((1,), jnp.int32) if last else after.reshape(1).astype(jnp.int32), h, back, wslot, now, gate]
    return pl.pallas_call(
        functools.partial(down_kernel, experts, blocks, last),
        out_shape=out if last else out + (jax.ShapeDtypeStruct(now.shape, bf16),),
        in_specs=[SM, VM, VM, VM, VM, VM] + ([] if last else [ANY]),
        out_specs=(VM, VM) if last else (VM, VM, VM),
        scratch_shapes=[pltpu.VMEM((blocks, experts * CAP, kb), bf16)]
        + ([] if last else [pltpu.SemaphoreType.DMA((experts, 2))]),
        compiler_params=pltpu.CompilerParams(vmem_limit_bytes=2 << 20),
        cost_estimate=pl.CostEstimate(
            flops=2 * experts * slots * kb * ff, bytes_accessed=2 * experts * kb * ff, transcendentals=0
        ),
    )(*args, *([] if last else [wd]))


def pair_kernel(chips, keep, got, base, *outs):
    for d in range(chips):
        v = keep[d].astype(f32) + got[d].astype(f32)
        if d == 0:
            base[...] = v
        else:
            outs[d - 1][...] = v.astype(bf16)


def pair_sum(keep, got):
    chips, toks, kb = keep.shape
    return pl.pallas_call(
        functools.partial(pair_kernel, chips),
        out_shape=(jax.ShapeDtypeStruct((toks, kb), f32),) + (jax.ShapeDtypeStruct((toks, kb), bf16),) * (chips - 1),
        in_specs=[VM, VM],
        out_specs=(VM,) * chips,
        compiler_params=pltpu.CompilerParams(vmem_limit_bytes=2 << 20),
        cost_estimate=pl.CostEstimate(flops=chips * toks * kb, bytes_accessed=8 * chips * toks * kb, transcendentals=0),
    )(keep, got)


def chip_kernel(base, *refs):
    v = base[...]
    for r in refs[:-1]:
        v = v + r[...].astype(f32)
    refs[-1][...] = v.astype(refs[-1].dtype)


def chip_sum(base, parts, dtype):
    return pl.pallas_call(
        chip_kernel,
        out_shape=jax.ShapeDtypeStruct(base.shape, dtype),
        in_specs=[VM] * (1 + len(parts)),
        out_specs=VM,
        compiler_params=pltpu.CompilerParams(vmem_limit_bytes=2 << 20),
        cost_estimate=pl.CostEstimate(flops=base.size, bytes_accessed=8 * base.size, transcendentals=0),
    )(base, *parts)


def down_chunk_plain(block, h, back, wslot, wd, kb):
    experts, _, _ = h.shape
    blocks, toks, _ = back.shape
    w = lax.dynamic_slice_in_dim(wd, block * kb, kb, axis=2)
    v = jnp.einsum("erf,efd->erd", h, w, preferred_element_type=f32)
    v = (v * wslot).astype(bf16).reshape(experts, blocks, CAP, kb).swapaxes(0, 1).reshape(blocks, experts * CAP, kb)
    y = jnp.einsum("jts,jsd->jtd", back, v, preferred_element_type=f32).astype(bf16)
    y = y.reshape(blocks // 2, 2, toks, kb)
    return y[:, 0], y[:, 1]


def layer(tokens, routes, router_weight, gate_weight, up_weight, down_weight):
    experts = gate_weight.shape[0]
    blocks = lax.axis_size("expert")
    nh = lax.axis_size("hidden")
    chips = blocks // 2
    toks, kb = tokens.shape
    e_at = lax.axis_index("expert")
    h_at = lax.axis_index("hidden")
    kernels = kb % 128 == 0 and toks % 128 == 0

    def over_core(v):
        return lax.ppermute(v, "expert", [(i, i ^ 1) for i in range(blocks)])

    def over_x(v, d):
        return lax.ppermute(v, "expert", [(i, i ^ (2 * d)) for i in range(blocks)])

    def over_z(v, k):
        return lax.ppermute(v, "hidden", [(i, i ^ k) for i in range(nh)])

    def spread(v, held=None):
        evens = [v] + [over_x(v, d) for d in range(1, chips)]
        crossed = [over_core(w) for w in evens]
        if held is not None:
            evens[0] = held
        return [w for pair in zip(evens, crossed) for w in pair]

    names = spread(routes.T)
    slices = {0: tokens}
    top = nh - 1
    low = top ^ 1
    direct = [1, top] if nh >= 4 else list(range(1, nh))
    for k in direct:
        slices[k] = over_z(tokens, k)
    for k in range(2, nh - 1):
        if k == low and top in slices:
            slices[k] = over_z(slices[top], 1)
        else:
            slices[k] = over_z(tokens, k)
    order = [0] + direct + [k for k in range(2, nh - 1) if k not in direct]

    router = router_weight.T
    if kernels:
        gate_weight, up_weight, down_weight = (
            pltpu.with_memory_space_constraint(w, pltpu.HBM) for w in (gate_weight, up_weight, down_weight)
        )
        held, router, weights = first_fetch(h_at, tokens, router, gate_weight, up_weight)
    else:
        held = tokens

    planned = plan if kernels else plan_plain
    sel, back, sign = planned(e_at * experts, names, experts, router_weight.shape[1])

    down_order = [k for k in range(nh - 1, 0, -1)] + [0]
    acc = None
    small = []
    for at, k in enumerate(order):
        if kernels and at >= 2:
            slices[k], small[at - 2] = lax.optimization_barrier((slices[k], small[at - 2]))
        xs = spread(slices[k], held if k == 0 else None)
        last = at == nh - 1
        if kernels:
            after = h_at ^ (down_order[0] if last else order[at + 1])
            ahead = (down_weight,) if last else (gate_weight, up_weight)
            *acc, weights = up_chunk(h_at ^ k, after, xs, sel, sign, router, weights, ahead, acc, last)
            small.append(acc[-1])
        else:
            acc = up_chunk_plain(h_at ^ k, xs, sel, sign, router, gate_weight, up_weight, acc, last)
    h, wslot = acc

    total = []
    sent = []
    for at, k in enumerate(down_order):
        if kernels:
            after = None if at == nh - 1 else h_at ^ down_order[at + 1]
            gate = sent[at - 2] if at >= 2 else wslot
            keep, send, *more = down_chunk(after, h, back, wslot, weights, down_weight, gate)
            weights = more[0] if more else None
        else:
            keep, send = down_chunk_plain(h_at ^ k, h, back, wslot, down_weight, kb)
        got = over_core(send)
        if kernels:
            base, *outs = pair_sum(keep, got)
        else:
            both = keep.astype(f32) + got.astype(f32)
            base, outs = both[0], [both[d].astype(bf16) for d in range(1, chips)]
        sent.append(outs[-1] if outs else keep)
        parts = [over_x(v, d + 1) for d, v in enumerate(outs)]
        if k == 0:
            total = [base] + [v.astype(f32) for v in parts] + total
            continue
        if kernels:
            mid = chip_sum(base, parts, bf16)
        else:
            mid = sum([v.astype(f32) for v in parts], base).astype(bf16)
        total.append(over_z(mid, k).astype(f32))
    total = functools.reduce(jnp.add, total)
    return total.astype(bf16)


def solution(mesh):
    return jax.shard_map(
        layer,
        mesh=mesh,
        in_specs=(
            P(("groups", "expert"), "hidden"),
            P(("groups", "expert"), None),
            P(),
            P("expert", None, "hidden"),
            P("expert", None, "hidden"),
            P("expert", "hidden", None),
        ),
        out_specs=P(("groups", "expert"), "hidden"),
        check_vma=False,
    )
```

```python
import functools
import jax
import jax.numpy as jnp
from jax import lax
from jax.experimental import pallas as pl
from jax.experimental.pallas import tpu as pltpu
from jax.sharding import PartitionSpec as P


CAP = 48
f32, bf16 = jnp.float32, jnp.bfloat16
VM = pl.BlockSpec(memory_space=pltpu.VMEM)
ANY = pl.BlockSpec(memory_space=pltpu.HBM)
SM = pl.BlockSpec(memory_space=pltpu.SMEM)


def silu_mul(gate, up):
    return (jax.nn.silu(gate) * up).astype(bf16)


def plan_kernel(blocks, experts, base, *refs):
    names, (sel_out, back_out, sign_out) = refs[:blocks], refs[blocks:]
    toks = names[0].shape[1]
    ahead = (lax.broadcasted_iota(jnp.int32, (toks, toks), 1) < lax.broadcasted_iota(jnp.int32, (toks, toks), 0)).astype(bf16)
    row = lax.broadcasted_iota(jnp.int32, (CAP, toks), 0)
    col = lax.broadcasted_iota(jnp.int32, (toks, CAP), 1)
    num = lax.broadcasted_iota(jnp.int32, (sign_out.shape[2], toks), 0)
    contract = (((1,), (1,)), ((), ()))
    for j in range(blocks):
        pair = names[j][...]
        for e in range(experts):
            own = base[0] + e
            mine = (pair[0:1] == own) | (pair[1:2] == own)
            flag = mine.astype(f32)
            wide = jnp.broadcast_to(flag, (8, toks)).astype(bf16)
            rank = lax.dot_general(wide, ahead, contract, preferred_element_type=f32)[0:1]
            rank = jnp.where(mine, rank, -1.0).astype(jnp.int32)
            sel_out[j, e * CAP : (e + 1) * CAP] = (rank == row).astype(f32).astype(bf16)
            deep = lax.dot_general(ahead, wide, contract, preferred_element_type=f32)[:, 0:1]
            eye = (lax.broadcasted_iota(jnp.int32, (toks, toks), 1) == lax.broadcasted_iota(jnp.int32, (toks, toks), 0)).astype(bf16)
            held = lax.dot_general(eye, wide, contract, preferred_element_type=f32)[:, 0:1]
            deep = jnp.where(held > 0.5, deep, -1.0).astype(jnp.int32)
            back_out[j, :, e * CAP : (e + 1) * CAP] = (deep == col).astype(f32).astype(bf16)
            other = pair[0:1] + pair[1:2] - own
            sign_out[j, e] = (num == own).astype(f32) - (num == other).astype(f32)


def plan(table, names, experts, count):
    blocks, toks = len(names), names[0].shape[1]
    return pl.pallas_call(
        functools.partial(plan_kernel, blocks, experts),
        out_shape=(
            jax.ShapeDtypeStruct((blocks, experts * CAP, toks), bf16),
            jax.ShapeDtypeStruct((blocks, toks, experts * CAP), bf16),
            jax.ShapeDtypeStruct((blocks, experts, count, toks), f32),
        ),
        in_specs=[SM] + [VM] * blocks,
        out_specs=(VM, VM, VM),
        compiler_params=pltpu.CompilerParams(vmem_limit_bytes=4 << 20),
        cost_estimate=pl.CostEstimate(flops=1 << 24, bytes_accessed=1 << 18, transcendentals=0),
    )(table[-1], *names)


def plan_plain(table, names, experts, count):
    base = table[-1][0]
    names = jnp.stack(names)
    blocks, _, toks = names.shape
    here = base + jnp.arange(experts, dtype=jnp.int32)
    mine = (names[:, None, :, :] == here[None, :, None, None]).any(axis=2)
    before = (jnp.arange(toks)[:, None] < jnp.arange(toks)[None, :]).astype(bf16)
    rank = jnp.dot(mine.astype(bf16).reshape(blocks * experts, toks), before, preferred_element_type=f32)
    rank = rank.astype(jnp.int32).reshape(blocks, experts, 1, toks)
    sel = mine[:, :, None, :] & (rank == jnp.arange(CAP, dtype=jnp.int32)[None, None, :, None])
    sel = sel.astype(bf16).reshape(blocks, experts * CAP, toks)
    num = jnp.arange(count, dtype=jnp.int32)[None, None, :, None]
    own = here[None, :, None, None]
    other = jnp.sum(names, axis=1)[:, None, None, :] - own
    return sel, sel.swapaxes(1, 2), (num == own).astype(f32) - (num == other).astype(f32)


def fetch_up(wg, wu, block, kb, out, sem, expert):
    at = pl.ds(pl.multiple_of(block * kb, 128), kb)
    return [pltpu.make_async_copy(w.at[expert, at], out.at[m], sem.at[m]) for m, w in enumerate((wg, wu))]


def fetch_down(wd, block, kb, out, sem):
    col = pl.ds(pl.multiple_of(block * kb, 128), kb)
    half = wd.shape[1] // 2
    copies = []
    for e in range(wd.shape[0]):
        for p in range(2):
            rows = pl.ds(p * half, half)
            copies.append(pltpu.make_async_copy(wd.at[e, rows, col], out.at[e, rows], sem.at[e, p]))
    return copies


def first_kernel(count, *refs):
    idx, (tokens, router, wg, wu, tok_out, router_out, w_out, sem, small) = refs[0], refs[count:]
    copies = [
        pltpu.make_async_copy(tokens, tok_out, small.at[0]),
        pltpu.make_async_copy(router, router_out, small.at[1]),
    ] + fetch_up(wg, wu, idx[0], tokens.shape[1], w_out, sem, 0)
    for c in copies:
        c.start()
    for c in copies:
        c.wait()


def first_fetch(table, tokens, router, wg, wu):
    ff = wg.shape[2]
    kb = tokens.shape[1]
    return pl.pallas_call(
        functools.partial(first_kernel, len(table)),
        out_shape=(
            jax.ShapeDtypeStruct(tokens.shape, bf16),
            jax.ShapeDtypeStruct(router.shape, bf16),
            jax.ShapeDtypeStruct((2, kb, ff), bf16),
        ),
        in_specs=[SM] * len(table) + [ANY] * 4,
        out_specs=(VM, VM, VM),
        scratch_shapes=[pltpu.SemaphoreType.DMA((2,)), pltpu.SemaphoreType.DMA((2,))],
        compiler_params=pltpu.CompilerParams(vmem_limit_bytes=1 << 20),
        cost_estimate=pl.CostEstimate(flops=0, bytes_accessed=4 * kb * ff, transcendentals=0),
    )(*table, tokens, router, wg, wu)


def up_kernel(first, last, blocks, experts, *refs):
    idx, refs = [r[0] for r in refs[:2]], list(refs[2:])
    xs, refs = refs[:blocks], refs[blocks:]
    sel, router, now, wg, wu = refs[:5]
    ahead = refs[5:6] if last else (wg, wu)
    refs = refs[6:] if last else refs[5:]
    if not first:
        g_in, u_in, l_in = refs[:3]
        refs = refs[3:]
    if last:
        sign, h_out, s_out, w_out = refs[:4]
        refs = refs[4:]
    else:
        g_out, u_out, l_out, w_out = refs[:4]
        refs = refs[4:]
    rows, sem, buf, own = refs
    kb = rows.shape[2]
    mine = [fetch_up(wg, wu, idx[0], kb, buf.at[e - 1], own.at[e - 1], e) for e in range(1, experts)]
    copies = fetch_down(*ahead, idx[1], kb, w_out, sem) if last else fetch_up(*ahead, idx[1], kb, w_out, sem, 0)
    for pair in mine:
        for c in pair:
            c.start()
    rt = router[:, pl.ds(pl.multiple_of(idx[0] * kb, 128), kb)]
    for j in range(blocks):
        x = xs[j][...]
        got = jnp.dot(sel[j], x, preferred_element_type=f32).astype(bf16)
        for e in range(experts):
            rows[e, j * CAP : (j + 1) * CAP] = got[e * CAP : (e + 1) * CAP]
        lt = lax.dot_general(rt, x, (((1,), (1,)), ((), ())), preferred_element_type=f32)
        lt = lt if first else l_in[j] + lt
        if not last:
            l_out[j] = lt
            continue
        for e in range(experts):
            w = jax.nn.sigmoid(jnp.sum(sign[j, e] * lt, axis=0, keepdims=True))
            at = sel[j, e * CAP : (e + 1) * CAP].astype(f32)
            s_out[e, j * CAP : (j + 1) * CAP] = jnp.sum(at * w, axis=1, keepdims=True)
    n_all = now.shape[2]
    step = min(512, n_all)
    turns = n_all // step

    def column(e, i, carry):
        sl = pl.ds(pl.multiple_of(i * step, step), step)
        x = rows[e]
        w = now if e == 0 else buf.at[e - 1]
        g = jnp.dot(x, w[0, :, sl], preferred_element_type=f32)
        u = jnp.dot(x, w[1, :, sl], preferred_element_type=f32)
        if not first:
            g = g_in[e, :, sl] + g
            u = u_in[e, :, sl] + u
        if last:
            h_out[e, :, sl] = silu_mul(g, u)
        else:
            g_out[e, :, sl] = g
            u_out[e, :, sl] = u
        return carry

    for e in range(experts):
        if e:
            for c in mine[e - 1]:
                c.wait()
        begin = 0
        if e == max(0, experts - 2):
            begin = turns // 2 if experts > 1 else 0
            lax.fori_loop(0, begin, functools.partial(column, e), 0)
            for c in copies:
                c.start()
        lax.fori_loop(begin, turns, functools.partial(column, e), 0)
    for c in copies:
        c.wait()


def up_chunk(table, spots, xs, sel, sign, router, now, ahead, acc, last):
    experts, _, ff = ahead[0].shape
    kb = xs[0].shape[1]
    blocks = len(xs)
    slots = blocks * CAP
    first = acc is None
    big = jax.ShapeDtypeStruct((experts, slots, ff), f32)
    lo = jax.ShapeDtypeStruct((blocks, router.shape[0], xs[0].shape[0]), f32)
    if last:
        out = (
            jax.ShapeDtypeStruct((experts, slots, ff), bf16),
            jax.ShapeDtypeStruct((experts, slots, 1), f32),
            jax.ShapeDtypeStruct((experts, ff, kb), bf16),
        )
    else:
        out = (big, big, lo, jax.ShapeDtypeStruct(now.shape, bf16))
    args = [*(table[i] for i in spots), *xs, sel, router, now, *ahead] + ([] if first else list(acc)) + ([sign] if last else [])
    n0 = 2 + blocks + 3 + len(ahead)
    alias = {} if first or last else {n0: 0, n0 + 1: 1, n0 + 2: 2}
    return pl.pallas_call(
        functools.partial(up_kernel, first, last, blocks, experts),
        out_shape=out,
        in_specs=[SM, SM] + [VM] * blocks + [VM] * 3 + [ANY] * len(ahead) + ([] if first else [VM] * 3) + ([VM] if last else []),
        out_specs=tuple([VM] * len(out)),
        scratch_shapes=[
            pltpu.VMEM((experts, slots, kb), bf16),
            pltpu.SemaphoreType.DMA((experts, 2) if last else (2,)),
            pltpu.VMEM((max(1, experts - 1), 2, kb, ff), bf16),
            pltpu.SemaphoreType.DMA((max(1, experts - 1), 2)),
        ],
        input_output_aliases=alias,
        compiler_params=pltpu.CompilerParams(vmem_limit_bytes=(2 << 20) + 4 * max(1, experts - 1) * kb * ff),
        cost_estimate=pl.CostEstimate(
            flops=4 * experts * slots * kb * ff,
            bytes_accessed=4 * experts * kb * ff,
            transcendentals=experts * slots * ff if last else 0,
        ),
    )(*args)


def up_chunk_plain(block, xs, sel, sign, router, wg, wu, acc, last):
    kb, experts, blocks = xs[0].shape[1], wg.shape[0], len(xs)
    x = jnp.stack(xs)
    rows = jnp.einsum("jst,jtd->jsd", sel, x, preferred_element_type=f32).astype(bf16)
    rows = rows.reshape(blocks, experts, CAP, kb).swapaxes(0, 1).reshape(experts, blocks * CAP, kb)
    cut = lambda w: lax.dynamic_slice_in_dim(w, block * kb, kb, axis=1)
    g = jnp.einsum("erd,edf->erf", rows, cut(wg), preferred_element_type=f32)
    u = jnp.einsum("erd,edf->erf", rows, cut(wu), preferred_element_type=f32)
    lo = jnp.einsum("nd,jtd->jnt", cut(router), x, preferred_element_type=f32)
    if acc is not None:
        g, u, lo = g + acc[0], u + acc[1], lo + acc[2]
    if not last:
        return g, u, lo
    weight = jax.nn.sigmoid(jnp.sum(sign * lo[:, None], axis=2))
    at = sel.astype(f32).reshape(blocks, experts, CAP, -1)
    wslot = jnp.sum(at * weight[:, :, None, :], axis=3).swapaxes(0, 1)
    return silu_mul(g, u), wslot.reshape(experts, blocks * CAP, 1)


def down_kernel(experts, blocks, last, *refs):
    idx, h_ref, back, wslot, now, _ = refs[:6]
    if last:
        keep, send, part = refs[6:]
        copies = []
    else:
        wd, keep, send, w_out, part, sem = refs[6:]
        copies = fetch_down(wd, idx[0], part.shape[2], w_out, sem)
    for c in copies:
        c.start()

    def product(e, carry):
        v = jnp.dot(h_ref[e], now[e], preferred_element_type=f32)
        v = (v * wslot[e]).astype(bf16)
        at = pl.ds(pl.multiple_of(e * CAP, CAP), CAP)
        for j in range(blocks):
            part[j, at] = v[j * CAP : (j + 1) * CAP]
        return carry

    lax.fori_loop(0, experts, product, 0)
    for j in range(blocks):
        y = jnp.dot(back[j], part[j], preferred_element_type=f32).astype(bf16)
        if j % 2 == 0:
            keep[j // 2] = y
        else:
            send[j // 2] = y
    for c in copies:
        c.wait()


def down_chunk(table, spot, h, back, wslot, now, wd, gate):
    experts, slots, ff = h.shape
    blocks, toks, _ = back.shape
    kb = now.shape[2]
    last = spot is None
    out = (jax.ShapeDtypeStruct((blocks // 2, toks, kb), bf16),) * 2
    args = [table[0 if last else spot], h, back, wslot, now, gate]
    return pl.pallas_call(
        functools.partial(down_kernel, experts, blocks, last),
        out_shape=out if last else out + (jax.ShapeDtypeStruct(now.shape, bf16),),
        in_specs=[SM, VM, VM, VM, VM, VM] + ([] if last else [ANY]),
        out_specs=(VM, VM) if last else (VM, VM, VM),
        scratch_shapes=[pltpu.VMEM((blocks, experts * CAP, kb), bf16)]
        + ([] if last else [pltpu.SemaphoreType.DMA((experts, 2))]),
        compiler_params=pltpu.CompilerParams(vmem_limit_bytes=2 << 20),
        cost_estimate=pl.CostEstimate(
            flops=2 * experts * slots * kb * ff, bytes_accessed=2 * experts * kb * ff, transcendentals=0
        ),
    )(*args, *([] if last else [wd]))


def pair_kernel(chips, keep, got, base, *outs):
    for d in range(chips):
        v = keep[d].astype(f32) + got[d].astype(f32)
        if d == 0:
            base[...] = v
        else:
            outs[d - 1][...] = v.astype(bf16)


def pair_sum(keep, got):
    chips, toks, kb = keep.shape
    return pl.pallas_call(
        functools.partial(pair_kernel, chips),
        out_shape=(jax.ShapeDtypeStruct((toks, kb), f32),) + (jax.ShapeDtypeStruct((toks, kb), bf16),) * (chips - 1),
        in_specs=[VM, VM],
        out_specs=(VM,) * chips,
        compiler_params=pltpu.CompilerParams(vmem_limit_bytes=2 << 20),
        cost_estimate=pl.CostEstimate(flops=chips * toks * kb, bytes_accessed=8 * chips * toks * kb, transcendentals=0),
    )(keep, got)


def chip_kernel(base, *refs):
    v = base[...]
    for r in refs[:-1]:
        v = v + r[...].astype(f32)
    refs[-1][...] = v.astype(refs[-1].dtype)


def chip_sum(base, parts, dtype):
    return pl.pallas_call(
        chip_kernel,
        out_shape=jax.ShapeDtypeStruct(base.shape, dtype),
        in_specs=[VM] * (1 + len(parts)),
        out_specs=VM,
        compiler_params=pltpu.CompilerParams(vmem_limit_bytes=2 << 20),
        cost_estimate=pl.CostEstimate(flops=base.size, bytes_accessed=8 * base.size, transcendentals=0),
    )(base, *parts)


def down_chunk_plain(block, h, back, wslot, wd, kb):
    experts, _, _ = h.shape
    blocks, toks, _ = back.shape
    w = lax.dynamic_slice_in_dim(wd, block * kb, kb, axis=2)
    v = jnp.einsum("erf,efd->erd", h, w, preferred_element_type=f32)
    v = (v * wslot).astype(bf16).reshape(experts, blocks, CAP, kb).swapaxes(0, 1).reshape(blocks, experts * CAP, kb)
    y = jnp.einsum("jts,jsd->jtd", back, v, preferred_element_type=f32).astype(bf16)
    y = y.reshape(blocks // 2, 2, toks, kb)
    return y[:, 0], y[:, 1]


def layer(tokens, routes, router_weight, gate_weight, up_weight, down_weight):
    experts = gate_weight.shape[0]
    blocks = lax.axis_size("expert")
    nh = lax.axis_size("hidden")
    chips = blocks // 2
    toks, kb = tokens.shape
    e_at = lax.axis_index("expert")
    h_at = lax.axis_index("hidden")
    table = [(h_at ^ k).astype(jnp.int32).reshape(1) for k in range(nh)]
    table.append((e_at * experts).astype(jnp.int32).reshape(1))
    kernels = kb % 128 == 0 and toks % 128 == 0

    def over_core(v):
        return lax.ppermute(v, "expert", [(i, i ^ 1) for i in range(blocks)])

    def over_x(v, d):
        return lax.ppermute(v, "expert", [(i, i ^ (2 * d)) for i in range(blocks)])

    def over_z(v, k):
        return lax.ppermute(v, "hidden", [(i, i ^ k) for i in range(nh)])

    def spread(v, held=None):
        evens = [v] + [over_x(v, d) for d in range(1, chips)]
        crossed = [over_core(w) for w in evens]
        if held is not None:
            evens[0] = held
        return [w for pair in zip(evens, crossed) for w in pair]

    names = spread(routes.T)
    slices = {0: tokens}
    top = nh - 1
    low = top ^ 1
    direct = [1, top] if nh >= 4 else list(range(1, nh))
    for k in direct:
        slices[k] = over_z(tokens, k)
    for k in range(2, nh - 1):
        if k == low and top in slices:
            slices[k] = over_z(slices[top], 1)
        else:
            slices[k] = over_z(tokens, k)
    order = [0] + direct + [k for k in range(2, nh - 1) if k not in direct]

    router = router_weight.T
    if kernels:
        gate_weight, up_weight, down_weight = (
            pltpu.with_memory_space_constraint(w, pltpu.HBM) for w in (gate_weight, up_weight, down_weight)
        )
        local = tokens
        router = pltpu.with_memory_space_constraint(router, pltpu.HBM)
        held, router, weights = first_fetch(table, local, router, gate_weight, up_weight)
    else:
        held = tokens

    planned = plan if kernels else plan_plain
    sel, back, sign = planned(table, names, experts, router_weight.shape[1])

    down_order = [k for k in range(nh - 1, 0, -1)] + [0]
    acc = None
    small = []
    for at, k in enumerate(order):
        if kernels and at >= 2:
            back_at = max(0, at - 3)
            slices[k], small[back_at] = lax.optimization_barrier((slices[k], small[back_at]))
        xs = spread(slices[k], held if k == 0 else None)
        last = at == nh - 1
        if kernels:
            spots = (k, down_order[0] if last else order[at + 1])
            ahead = (gate_weight, up_weight) + ((down_weight,) if last else ())
            *acc, weights = up_chunk(table, spots, xs, sel, sign, router, weights, ahead, acc, last)
            small.append(acc[-1])
        else:
            acc = up_chunk_plain(table[k][0], xs, sel, sign, router, gate_weight, up_weight, acc, last)
    h, wslot = acc

    total = []
    sent = []
    for at, k in enumerate(down_order):
        if kernels:
            spot = None if at == nh - 1 else down_order[at + 1]
            gate = sent[at - 2] if at >= 2 else wslot
            keep, send, *more = down_chunk(table, spot, h, back, wslot, weights, down_weight, gate)
            weights = more[0] if more else None
        else:
            keep, send = down_chunk_plain(table[k][0], h, back, wslot, down_weight, kb)
        got = over_core(send)
        if kernels:
            base, *outs = pair_sum(keep, got)
        else:
            both = keep.astype(f32) + got.astype(f32)
            base, outs = both[0], [both[d].astype(bf16) for d in range(1, chips)]
        sent.append(outs[-1] if outs else keep)
        parts = [over_x(v, d + 1) for d, v in enumerate(outs)]
        if k == 0:
            total = [base] + [v.astype(f32) for v in parts] + total
            continue
        if kernels:
            mid = chip_sum(base, parts, bf16)
        else:
            mid = sum([v.astype(f32) for v in parts], base).astype(bf16)
        total.append(over_z(mid, k).astype(f32))
    total = functools.reduce(jnp.add, total)
    return total.astype(bf16)


def solution(mesh):
    return jax.shard_map(
        layer,
        mesh=mesh,
        in_specs=(
            P(("groups", "expert"), "hidden"),
            P(("groups", "expert"), None),
            P(),
            P("expert", None, "hidden"),
            P("expert", None, "hidden"),
            P("expert", "hidden", None),
        ),
        out_specs=P(("groups", "expert"), "hidden"),
        check_vma=False,
    )
```

```python
import functools
import jax
import jax.numpy as jnp
from jax import lax
from jax.experimental import pallas as pl
from jax.experimental.pallas import tpu as pltpu
from jax.sharding import PartitionSpec as P


CAP = 48
f32, bf16 = jnp.float32, jnp.bfloat16
VM = pl.BlockSpec(memory_space=pltpu.VMEM)
ANY = pl.BlockSpec(memory_space=pltpu.HBM)
SM = pl.BlockSpec(memory_space=pltpu.SMEM)


def silu_mul(gate, up):
    return (jax.nn.silu(gate) * up).astype(bf16)


def plan_kernel(blocks, experts, base, *refs):
    names, (sel_out, back_out, sign_out) = refs[:blocks], refs[blocks:]
    toks = names[0].shape[1]
    ahead = (lax.broadcasted_iota(jnp.int32, (toks, toks), 1) < lax.broadcasted_iota(jnp.int32, (toks, toks), 0)).astype(bf16)
    row = lax.broadcasted_iota(jnp.int32, (CAP, toks), 0)
    col = lax.broadcasted_iota(jnp.int32, (toks, CAP), 1)
    num = lax.broadcasted_iota(jnp.int32, (sign_out.shape[2], toks), 0)
    contract = (((1,), (1,)), ((), ()))
    for j in range(blocks):
        pair = names[j][...]
        for e in range(experts):
            own = base[0] + e
            mine = (pair[0:1] == own) | (pair[1:2] == own)
            flag = mine.astype(f32)
            wide = jnp.broadcast_to(flag, (8, toks)).astype(bf16)
            rank = lax.dot_general(wide, ahead, contract, preferred_element_type=f32)[0:1]
            rank = jnp.where(mine, rank, -1.0).astype(jnp.int32)
            sel_out[j, e * CAP : (e + 1) * CAP] = (rank == row).astype(f32).astype(bf16)
            deep = lax.dot_general(ahead, wide, contract, preferred_element_type=f32)[:, 0:1]
            eye = (lax.broadcasted_iota(jnp.int32, (toks, toks), 1) == lax.broadcasted_iota(jnp.int32, (toks, toks), 0)).astype(bf16)
            held = lax.dot_general(eye, wide, contract, preferred_element_type=f32)[:, 0:1]
            deep = jnp.where(held > 0.5, deep, -1.0).astype(jnp.int32)
            back_out[j, :, e * CAP : (e + 1) * CAP] = (deep == col).astype(f32).astype(bf16)
            other = pair[0:1] + pair[1:2] - own
            sign_out[j, e] = (num == own).astype(f32) - (num == other).astype(f32)


def plan(table, names, experts, count):
    blocks, toks = len(names), names[0].shape[1]
    return pl.pallas_call(
        functools.partial(plan_kernel, blocks, experts),
        out_shape=(
            jax.ShapeDtypeStruct((blocks, experts * CAP, toks), bf16),
            jax.ShapeDtypeStruct((blocks, toks, experts * CAP), bf16),
            jax.ShapeDtypeStruct((blocks, experts, count, toks), f32),
        ),
        in_specs=[SM] + [VM] * blocks,
        out_specs=(VM, VM, VM),
        compiler_params=pltpu.CompilerParams(vmem_limit_bytes=4 << 20),
        cost_estimate=pl.CostEstimate(flops=1 << 24, bytes_accessed=1 << 18, transcendentals=0),
    )(table[-1], *names)


def plan_plain(table, names, experts, count):
    base = table[-1][0]
    names = jnp.stack(names)
    blocks, _, toks = names.shape
    here = base + jnp.arange(experts, dtype=jnp.int32)
    mine = (names[:, None, :, :] == here[None, :, None, None]).any(axis=2)
    before = (jnp.arange(toks)[:, None] < jnp.arange(toks)[None, :]).astype(bf16)
    rank = jnp.dot(mine.astype(bf16).reshape(blocks * experts, toks), before, preferred_element_type=f32)
    rank = rank.astype(jnp.int32).reshape(blocks, experts, 1, toks)
    sel = mine[:, :, None, :] & (rank == jnp.arange(CAP, dtype=jnp.int32)[None, None, :, None])
    sel = sel.astype(bf16).reshape(blocks, experts * CAP, toks)
    num = jnp.arange(count, dtype=jnp.int32)[None, None, :, None]
    own = here[None, :, None, None]
    other = jnp.sum(names, axis=1)[:, None, None, :] - own
    return sel, sel.swapaxes(1, 2), (num == own).astype(f32) - (num == other).astype(f32)


def fetch_up(wg, wu, block, kb, out, sem, expert):
    at = pl.ds(pl.multiple_of(block * kb, 128), kb)
    return [pltpu.make_async_copy(w.at[expert, at], out.at[m], sem.at[m]) for m, w in enumerate((wg, wu))]


def fetch_down(wd, block, kb, out, sem):
    col = pl.ds(pl.multiple_of(block * kb, 128), kb)
    half = wd.shape[1] // 2
    copies = []
    for e in range(wd.shape[0]):
        for p in range(2):
            rows = pl.ds(p * half, half)
            copies.append(pltpu.make_async_copy(wd.at[e, rows, col], out.at[e, rows], sem.at[e, p]))
    return copies


def first_kernel(count, *refs):
    idx, (tokens, router, wg, wu, tok_out, router_out, w_out, sem, small) = refs[0], refs[count:]
    copies = [
        pltpu.make_async_copy(tokens, tok_out, small.at[0]),
        pltpu.make_async_copy(router, router_out, small.at[1]),
    ] + fetch_up(wg, wu, idx[0], tokens.shape[1], w_out, sem, 0)
    for c in copies:
        c.start()
    for c in copies:
        c.wait()


def first_fetch(table, tokens, router, wg, wu):
    ff = wg.shape[2]
    kb = tokens.shape[1]
    return pl.pallas_call(
        functools.partial(first_kernel, len(table)),
        out_shape=(
            jax.ShapeDtypeStruct(tokens.shape, bf16),
            jax.ShapeDtypeStruct(router.shape, bf16),
            jax.ShapeDtypeStruct((2, kb, ff), bf16),
        ),
        in_specs=[SM] * len(table) + [ANY] * 4,
        out_specs=(VM, VM, VM),
        scratch_shapes=[pltpu.SemaphoreType.DMA((2,)), pltpu.SemaphoreType.DMA((2,))],
        compiler_params=pltpu.CompilerParams(vmem_limit_bytes=1 << 20),
        cost_estimate=pl.CostEstimate(flops=0, bytes_accessed=4 * kb * ff, transcendentals=0),
    )(*table, tokens, router, wg, wu)


def up_kernel(first, last, blocks, experts, *refs):
    idx, refs = [r[0] for r in refs[:2]], list(refs[2:])
    xs, refs = refs[:blocks], refs[blocks:]
    sel, router, now, wg, wu = refs[:5]
    ahead = refs[5:6] if last else (wg, wu)
    refs = refs[6:] if last else refs[5:]
    if not first:
        g_in, u_in, l_in = refs[:3]
        refs = refs[3:]
    if last:
        sign, h_out, s_out, w_out = refs[:4]
        refs = refs[4:]
    else:
        g_out, u_out, l_out, w_out = refs[:4]
        refs = refs[4:]
    rows, sem, buf, own = refs
    kb = rows.shape[2]
    mine = [fetch_up(wg, wu, idx[0], kb, buf.at[e - 1], own.at[e - 1], e) for e in range(1, experts)]
    copies = fetch_down(*ahead, idx[1], kb, w_out, sem) if last else fetch_up(*ahead, idx[1], kb, w_out, sem, 0)
    for pair in mine:
        for c in pair:
            c.start()
    rt = router[:, pl.ds(pl.multiple_of(idx[0] * kb, 128), kb)]
    for j in range(blocks):
        x = xs[j][...]
        got = jnp.dot(sel[j], x, preferred_element_type=f32).astype(bf16)
        for e in range(experts):
            rows[e, j * CAP : (j + 1) * CAP] = got[e * CAP : (e + 1) * CAP]
        lt = lax.dot_general(rt, x, (((1,), (1,)), ((), ())), preferred_element_type=f32)
        lt = lt if first else l_in[j] + lt
        if not last:
            l_out[j] = lt
            continue
        for e in range(experts):
            w = jax.nn.sigmoid(jnp.sum(sign[j, e] * lt, axis=0, keepdims=True))
            at = sel[j, e * CAP : (e + 1) * CAP].astype(f32)
            s_out[e, j * CAP : (j + 1) * CAP] = jnp.sum(at * w, axis=1, keepdims=True)
    n_all = now.shape[2]
    step = min(512, n_all)
    turns = n_all // step

    def column(e, i, carry):
        sl = pl.ds(pl.multiple_of(i * step, step), step)
        x = rows[e]
        w = now if e == 0 else buf.at[e - 1]
        g = jnp.dot(x, w[0, :, sl], preferred_element_type=f32)
        u = jnp.dot(x, w[1, :, sl], preferred_element_type=f32)
        if not first:
            g = g_in[e, :, sl] + g
            u = u_in[e, :, sl] + u
        if last:
            h_out[e, :, sl] = silu_mul(g, u)
        else:
            g_out[e, :, sl] = g
            u_out[e, :, sl] = u
        return carry

    for e in range(experts):
        if e:
            for c in mine[e - 1]:
                c.wait()
        begin = 0
        if e == max(0, experts - 2):
            begin = turns // 2 if experts > 1 else 0
            lax.fori_loop(0, begin, functools.partial(column, e), 0)
            for c in copies:
                c.start()
        lax.fori_loop(begin, turns, functools.partial(column, e), 0)
    for c in copies:
        c.wait()


def up_chunk(table, spots, xs, sel, sign, router, now, ahead, acc, last):
    experts, _, ff = ahead[0].shape
    kb = xs[0].shape[1]
    blocks = len(xs)
    slots = blocks * CAP
    first = acc is None
    big = jax.ShapeDtypeStruct((experts, slots, ff), f32)
    lo = jax.ShapeDtypeStruct((blocks, router.shape[0], xs[0].shape[0]), f32)
    if last:
        out = (
            jax.ShapeDtypeStruct((experts, slots, ff), bf16),
            jax.ShapeDtypeStruct((experts, slots, 1), f32),
            jax.ShapeDtypeStruct((experts, ff, kb), bf16),
        )
    else:
        out = (big, big, lo, jax.ShapeDtypeStruct(now.shape, bf16))
    args = [*(table[i] for i in spots), *xs, sel, router, now, *ahead] + ([] if first else list(acc)) + ([sign] if last else [])
    n0 = 2 + blocks + 3 + len(ahead)
    alias = {} if first or last else {n0: 0, n0 + 1: 1, n0 + 2: 2}
    return pl.pallas_call(
        functools.partial(up_kernel, first, last, blocks, experts),
        out_shape=out,
        in_specs=[SM, SM] + [VM] * blocks + [VM] * 3 + [ANY] * len(ahead) + ([] if first else [VM] * 3) + ([VM] if last else []),
        out_specs=tuple([VM] * len(out)),
        scratch_shapes=[
            pltpu.VMEM((experts, slots, kb), bf16),
            pltpu.SemaphoreType.DMA((experts, 2) if last else (2,)),
            pltpu.VMEM((max(1, experts - 1), 2, kb, ff), bf16),
            pltpu.SemaphoreType.DMA((max(1, experts - 1), 2)),
        ],
        input_output_aliases=alias,
        compiler_params=pltpu.CompilerParams(vmem_limit_bytes=(2 << 20) + 4 * max(1, experts - 1) * kb * ff),
        cost_estimate=pl.CostEstimate(
            flops=4 * experts * slots * kb * ff,
            bytes_accessed=4 * experts * kb * ff,
            transcendentals=experts * slots * ff if last else 0,
        ),
    )(*args)


def up_chunk_plain(block, xs, sel, sign, router, wg, wu, acc, last):
    kb, experts, blocks = xs[0].shape[1], wg.shape[0], len(xs)
    x = jnp.stack(xs)
    rows = jnp.einsum("jst,jtd->jsd", sel, x, preferred_element_type=f32).astype(bf16)
    rows = rows.reshape(blocks, experts, CAP, kb).swapaxes(0, 1).reshape(experts, blocks * CAP, kb)
    cut = lambda w: lax.dynamic_slice_in_dim(w, block * kb, kb, axis=1)
    g = jnp.einsum("erd,edf->erf", rows, cut(wg), preferred_element_type=f32)
    u = jnp.einsum("erd,edf->erf", rows, cut(wu), preferred_element_type=f32)
    lo = jnp.einsum("nd,jtd->jnt", cut(router), x, preferred_element_type=f32)
    if acc is not None:
        g, u, lo = g + acc[0], u + acc[1], lo + acc[2]
    if not last:
        return g, u, lo
    weight = jax.nn.sigmoid(jnp.sum(sign * lo[:, None], axis=2))
    at = sel.astype(f32).reshape(blocks, experts, CAP, -1)
    wslot = jnp.sum(at * weight[:, :, None, :], axis=3).swapaxes(0, 1)
    return silu_mul(g, u), wslot.reshape(experts, blocks * CAP, 1)


def down_kernel(experts, blocks, last, *refs):
    idx, h_ref, back, wslot, now, _ = refs[:6]
    if last:
        keep, send, part = refs[6:]
        copies = []
    else:
        wd, keep, send, w_out, part, sem = refs[6:]
        copies = fetch_down(wd, idx[0], part.shape[2], w_out, sem)
    for c in copies:
        c.start()

    def product(e, carry):
        v = jnp.dot(h_ref[e], now[e], preferred_element_type=f32)
        v = (v * wslot[e]).astype(bf16)
        at = pl.ds(pl.multiple_of(e * CAP, CAP), CAP)
        for j in range(blocks):
            part[j, at] = v[j * CAP : (j + 1) * CAP]
        return carry

    lax.fori_loop(0, experts, product, 0)
    for j in range(blocks):
        y = jnp.dot(back[j], part[j], preferred_element_type=f32).astype(bf16)
        if j % 2 == 0:
            keep[j // 2] = y
        else:
            send[j // 2] = y
    for c in copies:
        c.wait()


def down_chunk(table, spot, h, back, wslot, now, wd, gate):
    experts, slots, ff = h.shape
    blocks, toks, _ = back.shape
    kb = now.shape[2]
    last = spot is None
    out = (jax.ShapeDtypeStruct((blocks // 2, toks, kb), bf16),) * 2
    args = [table[0 if last else spot], h, back, wslot, now, gate]
    return pl.pallas_call(
        functools.partial(down_kernel, experts, blocks, last),
        out_shape=out if last else out + (jax.ShapeDtypeStruct(now.shape, bf16),),
        in_specs=[SM, VM, VM, VM, VM, VM] + ([] if last else [ANY]),
        out_specs=(VM, VM) if last else (VM, VM, VM),
        scratch_shapes=[pltpu.VMEM((blocks, experts * CAP, kb), bf16)]
        + ([] if last else [pltpu.SemaphoreType.DMA((experts, 2))]),
        compiler_params=pltpu.CompilerParams(vmem_limit_bytes=2 << 20),
        cost_estimate=pl.CostEstimate(
            flops=2 * experts * slots * kb * ff, bytes_accessed=2 * experts * kb * ff, transcendentals=0
        ),
    )(*args, *([] if last else [wd]))


def pair_kernel(chips, keep, got, base, *outs):
    for d in range(chips):
        v = keep[d].astype(f32) + got[d].astype(f32)
        if d == 0:
            base[...] = v
        else:
            outs[d - 1][...] = v.astype(bf16)


def pair_sum(keep, got):
    chips, toks, kb = keep.shape
    return pl.pallas_call(
        functools.partial(pair_kernel, chips),
        out_shape=(jax.ShapeDtypeStruct((toks, kb), f32),) + (jax.ShapeDtypeStruct((toks, kb), bf16),) * (chips - 1),
        in_specs=[VM, VM],
        out_specs=(VM,) * chips,
        compiler_params=pltpu.CompilerParams(vmem_limit_bytes=2 << 20),
        cost_estimate=pl.CostEstimate(flops=chips * toks * kb, bytes_accessed=8 * chips * toks * kb, transcendentals=0),
    )(keep, got)


def chip_kernel(base, *refs):
    v = base[...]
    for r in refs[:-1]:
        v = v + r[...].astype(f32)
    refs[-1][...] = v.astype(refs[-1].dtype)


def chip_sum(base, parts, dtype):
    return pl.pallas_call(
        chip_kernel,
        out_shape=jax.ShapeDtypeStruct(base.shape, dtype),
        in_specs=[VM] * (1 + len(parts)),
        out_specs=VM,
        compiler_params=pltpu.CompilerParams(vmem_limit_bytes=2 << 20),
        cost_estimate=pl.CostEstimate(flops=base.size, bytes_accessed=8 * base.size, transcendentals=0),
    )(base, *parts)


def down_chunk_plain(block, h, back, wslot, wd, kb):
    experts, _, _ = h.shape
    blocks, toks, _ = back.shape
    w = lax.dynamic_slice_in_dim(wd, block * kb, kb, axis=2)
    v = jnp.einsum("erf,efd->erd", h, w, preferred_element_type=f32)
    v = (v * wslot).astype(bf16).reshape(experts, blocks, CAP, kb).swapaxes(0, 1).reshape(blocks, experts * CAP, kb)
    y = jnp.einsum("jts,jsd->jtd", back, v, preferred_element_type=f32).astype(bf16)
    y = y.reshape(blocks // 2, 2, toks, kb)
    return y[:, 0], y[:, 1]


def layer(tokens, routes, router_weight, gate_weight, up_weight, down_weight):
    experts = gate_weight.shape[0]
    blocks = lax.axis_size("expert")
    nh = lax.axis_size("hidden")
    chips = blocks // 2
    toks, kb = tokens.shape
    e_at = lax.axis_index("expert")
    h_at = lax.axis_index("hidden")
    table = [(h_at ^ k).astype(jnp.int32).reshape(1) for k in range(nh)]
    table.append((e_at * experts).astype(jnp.int32).reshape(1))
    kernels = kb % 128 == 0 and toks % 128 == 0

    def over_core(v):
        return lax.ppermute(v, "expert", [(i, i ^ 1) for i in range(blocks)])

    def over_x(v, d):
        return lax.ppermute(v, "expert", [(i, i ^ (2 * d)) for i in range(blocks)])

    def over_z(v, k):
        return lax.ppermute(v, "hidden", [(i, i ^ k) for i in range(nh)])

    def spread(v, held=None):
        evens = [v] + [over_x(v, d) for d in range(1, chips)]
        crossed = [over_core(w) for w in evens]
        if held is not None:
            evens[0] = held
        return [w for pair in zip(evens, crossed) for w in pair]

    names = spread(routes.T)
    slices = {0: tokens}
    top = nh - 1
    low = top ^ 1
    direct = [1, top] if nh >= 4 else list(range(1, nh))
    for k in direct:
        slices[k] = over_z(tokens, k)
    for k in range(2, nh - 1):
        if k == low and top in slices:
            slices[k] = over_z(slices[top], 1)
        else:
            slices[k] = over_z(tokens, k)
    order = [0] + direct + [k for k in range(2, nh - 1) if k not in direct]

    router = router_weight.T
    if kernels:
        gate_weight, up_weight, down_weight = (
            pltpu.with_memory_space_constraint(w, pltpu.HBM) for w in (gate_weight, up_weight, down_weight)
        )
        local = tokens
        router = pltpu.with_memory_space_constraint(router, pltpu.HBM)
        held, router, weights = first_fetch(table, local, router, gate_weight, up_weight)
    else:
        held = tokens

    planned = plan if kernels else plan_plain
    sel, back, sign = planned(table, names, experts, router_weight.shape[1])

    down_order = ([low, top] if nh >= 4 else []) + [k for k in range(nh - 1, 0, -1) if nh < 4 or k not in (low, top)] + [0]
    acc = None
    small = []
    for at, k in enumerate(order):
        if kernels and at >= 2:
            back_at = max(0, at - 3)
            slices[k], small[back_at] = lax.optimization_barrier((slices[k], small[back_at]))
        xs = spread(slices[k], held if k == 0 else None)
        last = at == nh - 1
        if kernels:
            spots = (k, down_order[0] if last else order[at + 1])
            ahead = (gate_weight, up_weight) + ((down_weight,) if last else ())
            *acc, weights = up_chunk(table, spots, xs, sel, sign, router, weights, ahead, acc, last)
            small.append(acc[-1])
        else:
            acc = up_chunk_plain(table[k][0], xs, sel, sign, router, gate_weight, up_weight, acc, last)
    h, wslot = acc

    total = []
    sent = []
    passed = None
    for at, k in enumerate(down_order):
        if kernels:
            spot = None if at == nh - 1 else down_order[at + 1]
            gate = sent[at - 2] if at >= 2 else wslot
            keep, send, *more = down_chunk(table, spot, h, back, wslot, weights, down_weight, gate)
            weights = more[0] if more else None
        else:
            keep, send = down_chunk_plain(table[k][0], h, back, wslot, down_weight, kb)
        got = over_core(send)
        if kernels:
            base, *outs = pair_sum(keep, got)
        else:
            both = keep.astype(f32) + got.astype(f32)
            base, outs = both[0], [both[d].astype(bf16) for d in range(1, chips)]
        sent.append(outs[-1] if outs else keep)
        parts = [over_x(v, d + 1) for d, v in enumerate(outs)]
        if k == 0:
            total = [base] + [v.astype(f32) for v in parts] + total
            continue
        if k == top and passed is not None:
            parts.append(passed)
        if kernels:
            mid = chip_sum(base, parts, bf16)
        else:
            mid = sum([v.astype(f32) for v in parts], base).astype(bf16)
        if k == low and nh >= 4:
            passed = over_z(mid, 1)
        else:
            total.append(over_z(mid, k).astype(f32))
    total = functools.reduce(jnp.add, total)
    return total.astype(bf16)


def solution(mesh):
    return jax.shard_map(
        layer,
        mesh=mesh,
        in_specs=(
            P(("groups", "expert"), "hidden"),
            P(("groups", "expert"), None),
            P(),
            P("expert", None, "hidden"),
            P("expert", None, "hidden"),
            P("expert", "hidden", None),
        ),
        out_specs=P(("groups", "expert"), "hidden"),
        check_vma=False,
    )
```
